256 devices in a mesh: tile: 32 (over z_hi, y, core), lev: 8 (over x, z_lo).
Axes of the slice: x: 4, y: 4, z: 8 (z_hi: 4, z_lo: 2; z = z_hi * 2 + z_lo), core: 2. Of those that a mesh axis runs over, the one named last changes fastest.
Arguments:
- tracer_start: float32 [48, 2048, 720], P('lev', 'tile'), may hold values from -6 to 6
- wind_row: float32 [48, 2048, 720], P('lev', 'tile'), may hold values from -0.16 to 0.16
- wind_col: float32 [48, 2048, 720], P('lev', 'tile'), may hold values from -0.16 to 0.16
- diffusivity: float32 [48, 2048, 720], P('lev', 'tile'), may hold values from 0.01 to 0.16
- flux: float32 [11520, 128], P(('tile', 'lev')), may hold values from -6 to 6
- remap_weights: float32 [23040, 128, 128], P(('tile', 'lev')), may hold values from -0.5 to 0.5
- remap_tile: int32 [23040, 1], P(('tile', 'lev')), may hold values from 0 to 31; in each aligned block of 90 rows (0 to 89, 90 to 179, ...) at most 8 rows name the same one
- remap_block: int32 [23040], P(('tile', 'lev')), may hold values from 0 to 359
- profiles: float32 [64, 48], P(None, 'lev'), may hold values from -0.875 to 0.875
- sound_count: int32 [32], P('tile'), may hold values from 1 to 2048, 32768 in all
- sound_col: int32 [65536], P('tile'), may hold values from 0 to 46079
- sound_prof: int32 [65536], P('tile'), may hold values from 0 to 63
- sound_obs: float32 [65536], P('tile'), may hold values from -8 to 8
- sound_sigma: float32 [65536], P('tile'), may hold values from 0.5 to 2
Outputs:
- modeled: float32 [65536], P('tile')
- misfit: float32 [65536], P('tile')
- state_gradient: float32 [48, 2048, 720], P('lev', 'tile')
- flux_gradient: float32 [11520, 128], P(('tile', 'lev'))
The draws below stay inside these ranges and needn't reach their ends.
Inputs may be any that keep to these rules, and one draw needn't show every extreme that they name: `remap_tile`: within the (90) entries of one device no tile is named more than 8 times, a bound that some block reaches. `sound_count`: some tile has exactly 2048 live soundings.
All inputs are finite; a program needn't handle non-finite values. No bound on the sum of `sound_count` on one device may be relied on, other than what follows from the above.
Results may differ from the reference program's by a relative error of at most 0.0003.
Values sent between devices are 32-bit elements; how exact they have to be, the bound alone decides.
A program may use at most 128 MiB of HBM per device.

```python
import math
import jax
import jax.numpy as jnp
import numpy as np
from jax import lax

LEV = 48
COLS = 720
ROWS_DEV = 64
CB = 128
FB = 128
FBLK_DEV = 45
SLOT = 8
S_CAP = 2048
NPROF = 64
NROWS = 2048
CBLK_DEV = 360
NFBLK = 11520
NENT = 23040
NSOUND = 65536
N_TILE = 32


def plant(values, rng, least, top_value):
    dims = values.shape
    place = [jax.random.randint(jax.random.fold_in(rng, axis), (), 0, dims[axis]) for axis in range(len(dims))]
    values = values.at[tuple(place)].set(least)
    longest = dims.index(max(dims))
    place[longest] = (place[longest] + 1) % dims[longest]
    return values.at[tuple(place)].set(top_value)


def block_levels(rng, dims, pieces, low, high):
    factor_of = 1.0
    for position, blocks in pieces:
        draws = jax.random.uniform(jax.random.fold_in(jax.random.fold_in(rng, 6), position), (blocks,), jnp.float32, low / len(pieces), high / len(pieces))
        factor_of = factor_of * jnp.repeat(jnp.exp(draws), dims[position] // blocks).reshape((-1,) + (1,) * (len(dims) - 1 - position))
    return factor_of


def profile(count, total, bound, lean):
    weights = [(1 << 20) // math.isqrt(rank ** lean) + 1 for rank in range(2, count + 1)]
    spare, holding = total - bound - (count - 1), [1] * (count - 1)
    while spare > 0:
        free = [i for i in range(count - 1) if holding[i] < bound]
        mass, left = sum([weights[i] for i in free]), spare
        for i in free:
            more = min(bound - holding[i], max(1, left * weights[i] // mass), spare)
            holding[i] = holding[i] + more
            spare = spare - more
    return np.array([bound] + holding)


def uneven_parts(own_key, number_of, total, bound, skew):
    if number_of == 2:
        one = jax.random.randint(own_key, (), max(1, total - bound), min(bound, total - 1) + 1)
        return jnp.stack([one, total - one])
    sizes = jnp.asarray(profile(number_of, total, bound, skew), jnp.int32)
    pairs = (number_of - 1) // 2
    giver, receiver = sizes[1:1 + 2 * pairs:2], sizes[2:2 + 2 * pairs:2]
    slack = jnp.minimum(giver - 1, bound - receiver)
    moved = jax.random.randint(jax.random.fold_in(own_key, 1), (pairs,), 0, 1 << 20) % (slack + 1)
    sizes = sizes.at[1:1 + 2 * pairs:2].set(giver - moved).at[2:2 + 2 * pairs:2].set(receiver + moved)
    return sizes[jax.random.permutation(jax.random.fold_in(own_key, 2), number_of)]


def shared_out(stream_key, own, number, rows, number_of, top, most, skew):
    sequence = jax.random.permutation(stream_key, number_of)
    packed, ordinary = portions_of(number_of, rows * top, most, skew, True), portions_of(number_of, rows * top, most, skew, False)
    places = jnp.arange(number_of)

    def named(tallies, turn):
        used = int((tallies > 0).sum())
        fixed = max(1, used // 4)
        moved = fixed + (places - fixed + turn * (used - fixed)) % max(1, number_of - fixed)
        return jnp.zeros((number_of,), jnp.int32).at[sequence[jnp.where(places < fixed, places, moved)]].set(jnp.asarray(tallies, jnp.int32))

    tallies = jnp.where(number % 4 == 0, named(packed, number // 4), named(ordinary, number - number // 4 - 1))
    mixed = jax.random.permutation(jax.random.fold_in(own, 3), number_of)
    donor, receiver = mixed[0:number_of // 2 * 2:2], mixed[1:number_of // 2 * 2:2]
    slack = jnp.minimum(tallies[donor] - 1, most - tallies[receiver]) // 2
    slack = jnp.where((donor == sequence[0]) | (receiver == sequence[0]) | (tallies[receiver] == 0), 0, jnp.maximum(slack, 0))
    moved = jax.random.randint(jax.random.fold_in(own, 4), (number_of // 2,), 0, 1 << 20) % (slack + 1)
    tallies = tallies.at[donor].add(-moved).at[receiver].add(moved)
    members = jnp.searchsorted(jnp.cumsum(tallies), jnp.arange(rows * top), side="right").astype(jnp.int32)
    grid = members.reshape(top, rows).T
    grid = grid[jax.random.permutation(jax.random.fold_in(own, 1), rows)]
    turn = jax.random.randint(jax.random.fold_in(own, 2), (rows, 1), 0, top)
    return jnp.take_along_axis(grid, (jnp.arange(top)[None, :] + turn) % top, axis=1)


def portions_of(number_of, total, bound, skew, full):
    portions = [(1 << 20) // math.isqrt(standing ** skew) + 1 for standing in range(1, number_of + 1)]
    largest = bound if full else min(bound, max(-(-total // number_of), total * portions[0] // sum(portions)))
    least = 1 if total - largest >= number_of - 1 else 0
    holding, spare = [largest] + [least] * (number_of - 1), total - largest - least * (number_of - 1)
    while spare > 0:
        candidates = [i for i in range(1, number_of) if holding[i] < largest] or [i for i in range(1, number_of) if holding[i] < bound]
        whole, remaining = sum([portions[i] for i in candidates]), spare
        for i in candidates:
            more = min(bound - holding[i], max(1, remaining * portions[i] // whole), spare)
            holding[i] = holding[i] + more
            spare = spare - more
    return np.array(holding)


def noise(stream_key, shape, spread, most, cuts=(), held_as=jnp.bfloat16):
    factor_of = block_levels(stream_key, shape, cuts, -0.22, 0.18) if cuts else 1.0
    result = jax.random.normal(stream_key, shape, jnp.float32) * spread * factor_of
    return jnp.minimum(jnp.maximum(result, -most), most).astype(held_as)


def setup_inputs(seed: int = 0) -> dict:
    seeds = jax.random.split(jax.random.key(seed), 15)
    tracer_start = noise(seeds[0], (LEV, NROWS, COLS), 1.0, 6.0, ((0, 8), (1, 32)), jnp.float32)
    wind_row = jnp.clip(jax.random.uniform(seeds[1], (LEV, NROWS, COLS), jnp.float32, -0.16, 0.16) * block_levels(seeds[1], (LEV, NROWS, COLS), ((0, 8), (1, 32)), -0.4, 0.0), -0.16, 0.16)
    wind_col = jnp.clip(jax.random.uniform(seeds[2], (LEV, NROWS, COLS), jnp.float32, -0.16, 0.16) * block_levels(seeds[2], (LEV, NROWS, COLS), ((0, 8), (1, 32)), -0.4, 0.0), -0.16, 0.16)
    diffusivity = jnp.clip(0.01 + 0.149999997 * jax.random.uniform(seeds[3], (LEV, NROWS, COLS), jnp.float32) ** block_levels(seeds[3], (LEV, NROWS, COLS), ((0, 8), (1, 32)), -0.2, 0.2), 0.01, 0.16)
    flux = noise(seeds[4], (NFBLK, FB), 1.0, 6.0, ((0, 256),), jnp.float32)
    remap_weights = noise(seeds[5], (NENT, CB, FB), FB ** -0.5, 0.5, ((0, 256),), jnp.float32)
    remap_tile_keys = jax.random.split(jax.random.fold_in(seeds[6], 1), NENT // (2 * FBLK_DEV))
    remap_tile_turns = jax.random.permutation(jax.random.fold_in(seeds[6], 3), NENT // (2 * FBLK_DEV))
    remap_tile = jax.vmap(lambda own, number: shared_out(jax.random.fold_in(seeds[6], 2), own, number, 2 * FBLK_DEV, N_TILE, 1, SLOT, 2))(remap_tile_keys, remap_tile_turns).reshape((NENT, 1))
    remap_block = plant(jax.random.randint(seeds[7], (NENT,), 0, CBLK_DEV), jax.random.fold_in(seeds[7], 1), 0, CBLK_DEV - 1).astype(jnp.int32)
    profiles = noise(seeds[8], (NPROF, LEV), LEV ** -0.5, 0.875, ((1, 8),), jnp.float32)
    sound_count = uneven_parts(seeds[9], N_TILE, N_TILE * S_CAP // 2, S_CAP, 2).astype(jnp.int32)
    sound_col = plant(jax.random.randint(seeds[10], (NSOUND,), 0, ROWS_DEV * COLS), jax.random.fold_in(seeds[10], 1), 0, (ROWS_DEV * COLS) - 1).astype(jnp.int32)
    sound_prof = plant(jax.random.randint(seeds[11], (NSOUND,), 0, NPROF), jax.random.fold_in(seeds[11], 1), 0, NPROF - 1).astype(jnp.int32)
    sound_obs = noise(seeds[12], (NSOUND,), 1.5, 8.0, ((0, 32),), jnp.float32)
    sound_sigma = jnp.clip(jnp.exp(math.log(2.0) - 1.3862944 * jax.random.uniform(seeds[13], (NSOUND,), jnp.float32) ** block_levels(seeds[13], (NSOUND,), ((0, 32),), -0.2, 0.2)), 0.5, 2.0)
    return {"tracer_start": tracer_start, "wind_row": wind_row, "wind_col": wind_col, "diffusivity": diffusivity, "flux": flux, "remap_weights": remap_weights, "remap_tile": remap_tile, "remap_block": remap_block, "profiles": profiles, "sound_count": sound_count, "sound_col": sound_col, "sound_prof": sound_prof, "sound_obs": sound_obs, "sound_sigma": sound_sigma}


highest = lax.Precision.HIGHEST


def earlier(array, axis):
    first = jnp.zeros_like(lax.slice_in_dim(array, 0, 1, axis=axis))
    rest = lax.slice_in_dim(array, 0, array.shape[axis] - 1, axis=axis)
    return jnp.concatenate([first, rest], axis=axis)


def later(array, axis):
    last = jnp.zeros_like(lax.slice_in_dim(array, 0, 1, axis=axis))
    rest = lax.slice_in_dim(array, 1, array.shape[axis], axis=axis)
    return jnp.concatenate([rest, last], axis=axis)


def apply_step(field, above, below, upper, lower, coeffs, adjoint):
    rise, rise_low, cross, cross_left, mixing, mixing_low = coeffs
    right = jnp.roll(field, -1, axis=2)
    left = jnp.roll(field, 1, axis=2)
    rise_pos = jnp.maximum(rise, 0.0)
    rise_neg = jnp.minimum(rise, 0.0)
    low_pos = jnp.maximum(rise_low, 0.0)
    low_neg = jnp.minimum(rise_low, 0.0)
    cross_pos = jnp.maximum(cross, 0.0)
    cross_neg = jnp.minimum(cross, 0.0)
    left_pos = jnp.maximum(cross_left, 0.0)
    left_neg = jnp.minimum(cross_left, 0.0)
    diffusion = mixing * (above - field) - mixing_low * (field - below)
    if adjoint:
        rows_term = rise_pos * (upper - field) - low_neg * (lower - field)
        cols_term = cross_pos * (right - field) - left_neg * (left - field)
    else:
        rows_term = low_pos * lower + low_neg * field - rise_pos * field - rise_neg * upper
        cols_term = left_pos * left + left_neg * field - cross_pos * field - cross_neg * right
    return field + rows_term + cols_term + diffusion


def transport(field, coeffs, adjoint):
    return apply_step(field, later(field, 0), earlier(field, 0), later(field, 1), earlier(field, 1), coeffs, adjoint)


def reference(tracer_start, wind_row, wind_col, diffusivity, flux, remap_weights, remap_tile, remap_block, profiles, sound_count, sound_col, sound_prof, sound_obs, sound_sigma):
    rise = wind_row.at[:, -1, :].set(0.0)
    rise_low = earlier(rise, 1)
    cross_left = jnp.roll(wind_col, 1, axis=2)
    mixing = diffusivity.at[-1].set(0.0)
    mixing_low = earlier(mixing, 0)
    coeffs = (rise, rise_low, wind_col, cross_left, mixing, mixing_low)

    target = remap_tile[:, 0] * CBLK_DEV + remap_block
    flux_rep = jnp.repeat(flux, 2, axis=0)
    contrib = jnp.einsum("ecf,ef->ec", remap_weights, flux_rep, precision=highest, preferred_element_type=jnp.float32)
    surface = jax.ops.segment_sum(contrib, target, num_segments=N_TILE * CBLK_DEV).reshape(NROWS, COLS)

    state = transport(tracer_start, coeffs, False)
    state = state.at[0].add(surface)
    state = transport(state, coeffs, False)
    state = state.at[0].add(surface)

    slots = jnp.arange(N_TILE * S_CAP, dtype=jnp.int32)
    owner = slots // S_CAP
    live = (slots % S_CAP) < sound_count[owner]
    cell = owner * (ROWS_DEV * COLS) + sound_col
    flat = state.reshape(LEV, NROWS * COLS)
    values = flat[:, cell]
    weights = profiles[sound_prof]
    column = jnp.sum(weights * values.T, axis=1)
    modeled = jnp.where(live, column, 0.0)
    scaled = (column - sound_obs) / sound_sigma
    size_abs = jnp.abs(scaled)
    huber = jnp.where(size_abs <= 1.0, 0.5 * scaled * scaled, size_abs - 0.5)
    misfit = jnp.where(live, huber, 0.0)
    slope = jnp.where(live, jnp.clip(scaled, -1.0, 1.0) / sound_sigma, 0.0)

    adjoint_two = jnp.zeros((LEV, NROWS * COLS), jnp.float32).at[:, cell].add((weights * slope[:, None]).T)
    adjoint_two = adjoint_two.reshape(LEV, NROWS, COLS)
    adjoint_one = transport(adjoint_two, coeffs, True)
    state_gradient = transport(adjoint_one, coeffs, True)

    surface_bar = (adjoint_two[0] + adjoint_one[0]).reshape(N_TILE * CBLK_DEV, CB)
    picked = surface_bar[target]
    per_entry = jnp.einsum("ecf,ec->ef", remap_weights, picked, precision=highest, preferred_element_type=jnp.float32)
    flux_gradient = per_entry.reshape(-1, 2, FB).sum(axis=1)
    return (modeled, misfit, state_gradient, flux_gradient)
```

```python
import functools

import jax
import jax.numpy as jnp
from jax import lax
from jax.experimental import pallas as pl
from jax.experimental.pallas import tpu as pltpu
from jax.sharding import PartitionSpec as P

MESH = pl.DeviceIdType.MESH
f32 = jnp.float32
bf16 = jnp.bfloat16
NT_DIMS = (((1,), (1,)), ((), ()))
SLOT = 8
CH = 256


def split2(x):
    hi = x.astype(bf16)
    return hi, (x - hi.astype(f32)).astype(bf16)


def dot(a, b):
    return jnp.dot(a, b, preferred_element_type=f32)


def dot_nt(a, b):
    return lax.dot_general(a, b, NT_DIMS, preferred_element_type=f32)


def iota(shape, dim):
    return lax.broadcasted_iota(jnp.int32, shape, dim)


def rcopy(src, dst, ss, rs, dev):
    return pltpu.make_async_remote_copy(
        src_ref=src, dst_ref=dst, send_sem=ss, recv_sem=rs, device_id=dev, device_id_type=MESH
    )


def sizes_of(shapes):
    levels, rows, cols = shapes[0]
    return levels, rows, cols


def body(
    dims,
    tr_h, wr_h, wc_h, df_h, w_h,
    flux, tcol, trow, brow, prof, cnt, scol, sprof, sobs, ssig,
    modeled, misfit, grad, fgrad,
    t_v, wr, wc, mx, w_v, wcat, contrib, sbuf, rbuf, sid, rid, pbuf,
    pk0u, pk0d, rb0lo, rb0hi, pk1u, pk1d, rb1lo, rb1hi, pk2u, pk2d, rb2lo, rb2hi,
    pk3u, pk3d, rb3lo, rb3hi,
    ct, amat, gmat, s1, s2, rowi, w8, qv, cbuf, slope_v, a2, bs, a1, surf6, blk, bout, bin_, picked,
    sem_in, s_lv, r_lv, s_pr, r_pr, s_r0, r_r0, s_a, r_a, s_i, r_i, s_q, r_q,
    s_r1, r_r1, s_c, r_c, s_r2, r_r2, s_l1, r_l1, s_r3, r_r3, s_b, r_b,
):
    NT, NL, L, R, C, S, NE, CPG = dims
    NP = NE // 2
    NB = R * C // 128
    SL = NT * SLOT
    NG = max(1, NT // 16)
    LG = min(128, SL)
    NCH = NP // CPG
    t = lax.axis_index("tile")
    l = lax.axis_index("lev")
    tup, tdn = lax.rem(t + 1, NT), lax.rem(t + NT - 1, NT)
    lup, ldn = lax.rem(l + 1, NL), lax.rem(l + NL - 1, NL)

    barrier = pltpu.get_barrier_semaphore()

    def sig_t(d, _):
        pl.semaphore_signal(barrier, inc=1, device_id={"tile": lax.rem(t + d, NT)}, device_id_type=MESH)
        return 0

    def sig_l(d, _):
        pl.semaphore_signal(barrier, inc=1, device_id={"lev": lax.rem(l + d, NL)}, device_id_type=MESH)
        return 0

    lax.fori_loop(1, NT, sig_t, 0)
    lax.fori_loop(1, NL, sig_l, 0)

    loads = [
        pltpu.make_async_copy(tr_h, t_v.at[pl.ds(1, L)], sem_in.at[0]),
        pltpu.make_async_copy(wr_h, wr, sem_in.at[1]),
        pltpu.make_async_copy(wc_h, wc, sem_in.at[2]),
        pltpu.make_async_copy(df_h, mx.at[pl.ds(1, L)], sem_in.at[3]),
    ]

    def wload(i):
        part = pl.ds(2 * CPG * i, 2 * CPG)
        return pltpu.make_async_copy(w_h.at[part], w_v.at[part], sem_in.at[4 + i])

    loads[0].start()
    loads[1].start()
    for i in range(NCH):
        wload(i).start()
    loads[2].start()
    loads[3].start()

    pl.semaphore_wait(barrier, NT - 1 + NL - 1)

    planes = [
        rcopy(tr_h.at[L - 1], t_v.at[0], s_lv.at[0], r_lv.at[0], {"lev": lup}),
        rcopy(tr_h.at[0], t_v.at[L + 1], s_lv.at[1], r_lv.at[1], {"lev": ldn}),
        rcopy(df_h.at[L - 1], mx.at[0], s_lv.at[2], r_lv.at[2], {"lev": lup}),
    ]
    for c in planes:
        c.start()

    def prof_copy(to, slot):
        return rcopy(prof, pbuf.at[slot], s_pr.at[to], r_pr.at[slot], {"lev": to})

    def prof_send(d, _):
        to = lax.rem(l + d, NL)
        prof_copy(to, l).start()
        return 0

    lax.fori_loop(1, NL, prof_send, 0)
    pbuf[l] = prof[...]

    def pair_copies(pku, pkd, lo, hi, ss, rs):
        return [
            rcopy(pku, lo, ss.at[0], rs.at[0], {"tile": tup}),
            rcopy(pkd, hi, ss.at[1], rs.at[1], {"tile": tdn}),
        ]

    loads[0].wait()
    loads[1].wait()
    top = jnp.where(t == NT - 1, 0.0, 1.0).astype(f32)
    low_ok = jnp.where(t == 0, 0.0, 1.0).astype(f32)
    pk0u[...] = jnp.zeros_like(pk0u)
    pk0d[...] = jnp.zeros_like(pk0d)
    for k in range(L):
        wr[k, R - 1 : R, :] = wr[k, R - 1 : R, :] * top
        pk0u[k : k + 1, :] = t_v[k + 1, R - 1 : R, :]
        pk0u[8 + k : 9 + k, :] = wr[k, R - 1 : R, :]
        pk0d[k : k + 1, :] = t_v[k + 1, 0:1, :]
    rows0 = pair_copies(pk0u, pk0d, rb0lo, rb0hi, s_r0, r_r0)
    for c in rows0:
        c.start()

    r16 = iota((16, 2 * 128), 0)
    l16 = iota((16, 2 * 128), 1)

    def contrib_step(i, _):
        wload(i).wait()
        outs = []
        for p in range(CPG):
            f = i * CPG + p
            w2 = w_v[pl.ds(2 * f, 2)].reshape(256, 128)
            hi, lo = split2(w2)
            wc2 = jnp.concatenate([hi, lo], axis=1)
            wcat[f] = wc2
            row = flux[pl.ds(f, 1), :]
            fh = row.astype(bf16).astype(f32)
            fl = row - fh
            both = jnp.where(
                r16 == 0,
                jnp.concatenate([fh, fh], axis=1),
                jnp.where((r16 == 1) & (l16 < 128), jnp.concatenate([fl, fl], axis=1), 0.0),
            )
            got = dot_nt(both.astype(bf16), wc2)
            outs.append(got[0:1] + got[1:2])
        for p in range(CPG):
            f = i * CPG + p
            contrib[pl.ds(2 * f, 1), :] = outs[p][:, :128]
            contrib[pl.ds(2 * f + 1, 1), :] = outs[p][:, 128:]
        return 0

    lax.fori_loop(0, NCH, contrib_step, 0)

    tr_row, tr_col = trow[...], tcol[...]
    same = tr_col == tr_row
    sub, lan = iota((NE, NE), 0), iota((NE, NE), 1)
    rank_row = jnp.sum(jnp.where(same & (sub < lan), 1.0, 0.0), axis=0, keepdims=True)
    rank_col = jnp.sum(jnp.where(same & (lan < sub), 1.0, 0.0), axis=1, keepdims=True)
    sel_row = tr_row * SLOT + rank_row.astype(jnp.int32)
    sel_col = tr_col * SLOT + rank_col.astype(jnp.int32)
    place = jnp.where(iota((SL, NE), 0) == sel_row, 1.0, 0.0).astype(bf16)
    ch, cl = split2(contrib[...])
    slots = dot(place, ch) + dot(place, cl)
    sbuf[...] = slots.reshape(NT, SLOT, 128)
    base = lax.rem(t, 16) * SLOT
    spot = jnp.where(iota((NE, 128), 1) == rank_col.astype(jnp.int32) + base, 1.0, 0.0).astype(bf16)
    at_tile = iota((NT, NE), 0) == tr_row
    bid = brow[...] + 1
    bid_hi = jnp.where(bid >= 256, 256.0, 0.0)
    bid_lo = bid.astype(f32) - bid_hi
    ids = dot(jnp.where(at_tile, bid_hi, 0.0).astype(bf16), spot) + dot(
        jnp.where(at_tile, bid_lo, 0.0).astype(bf16), spot
    )
    sid[...] = ids.reshape(NT, 1, 128)

    def a_copy(to, slot):
        return rcopy(sbuf.at[to], rbuf.at[slot], s_a.at[to], r_a.at[slot], {"tile": to})

    def i_copy(to, slot):
        return rcopy(sid.at[to], rid.at[slot], s_i.at[to], r_i.at[slot], {"tile": to})

    def a2a_send(d, _):
        to = lax.rem(t + d, NT)
        i_copy(to, t).start()
        a_copy(to, t).start()
        return 0

    lax.fori_loop(1, NT, a2a_send, 0)
    rbuf[t] = sbuf[t]
    rid[t] = sid[t]

    cell = scol[...]
    row_s = ((cell.astype(f32) + 0.5) * (1.0 / C)).astype(jnp.int32)
    col_s = cell - row_s * C
    rowi[...] = row_s

    def ct_step(i, _):
        off = pl.multiple_of(i * 16, 16)
        ct[pl.ds(off, 16), :] = jnp.where(iota((16, S), 0) + off == col_s, 1.0, 0.0).astype(bf16)
        return 0

    lax.fori_loop(0, ct.shape[0] // 16, ct_step, 0)

    def prof_wait(d, _):
        src = lax.rem(l + d, NL)
        prof_copy(src, src).wait_recv()
        return 0

    lax.fori_loop(1, NL, prof_wait, 0)
    pm = jnp.concatenate([pbuf[ldn][L - 1 : L], pbuf[l][0:L], pbuf[lup][0:1]], axis=0)
    p_hi = pm.astype(bf16)
    rest = pm - p_hi.astype(f32)
    p_mid = rest.astype(bf16)
    p_lo = rest - p_mid.astype(f32)
    pm3 = jnp.concatenate([p_hi.astype(f32), p_mid.astype(f32), p_lo, jnp.zeros_like(p_lo)], axis=0).astype(bf16)
    pick = jnp.where(iota((128, S), 0) == sprof[...], 1.0, 0.0).astype(bf16)
    w24 = dot(pm3, pick)
    w8[...] = w24[0:8] + w24[8:16] + w24[16:24]

    loads[2].wait()
    loads[3].wait()
    for c in rows0:
        c.wait_recv()
    rb0lo[8:16, :] = rb0lo[8:16, :] * low_ok
    mx[L] = mx[L] * jnp.where(l == NL - 1, 0.0, 1.0).astype(f32)
    QR = 80 + 3 * R

    def put_g(at, value, total):
        n = value.shape[0]
        hi, lo = split2(value)
        gmat[at : at + n, :] = hi
        gmat[total + at : total + at + n, :] = lo

    RS = R + 16
    rise_x = jnp.concatenate([rb0lo[8:9, :], wr[0], jnp.zeros((15, C), f32)], axis=0)
    wc0 = wc[0]
    QT = RS + 3 * R
    put_g(0, rise_x, QT)
    put_g(RS, wc0, QT)
    put_g(RS + R, jnp.roll(wc0, 1, axis=1), QT)
    put_g(RS + 2 * R, mx[1], QT)
    idx = iota((RS, CH), 0)
    idr = iota((R, CH), 0)

    def q_step(j, _):
        lanes = pl.ds(pl.multiple_of(j * CH, CH), CH)
        v2 = dot(gmat[0 : 2 * QT, :], ct[0:C, lanes])
        v = v2[:QT] + v2[QT:]
        r = rowi[:, lanes]
        vx = v[:RS]
        rise_s = jnp.sum(jnp.where(idx == r + 1, vx, 0.0), axis=0, keepdims=True)
        low_s = jnp.sum(jnp.where(idx == r, vx, 0.0), axis=0, keepdims=True)
        mine = idr == r

        def at(o):
            return jnp.sum(jnp.where(mine, v[o : o + R], 0.0), axis=0, keepdims=True)

        cross_s, left_s, mix_s = at(RS), at(RS + R), at(RS + 2 * R)
        p0, p1 = w8[1:2, lanes], w8[2:3, lanes]
        low_neg, low_pos = jnp.minimum(low_s, 0.0), jnp.maximum(low_s, 0.0)
        left_neg, left_pos = jnp.minimum(left_s, 0.0), jnp.maximum(left_s, 0.0)
        self_c = 2.0 + low_neg - jnp.maximum(rise_s, 0.0) + left_neg - jnp.maximum(cross_s, 0.0) - mix_s
        qv[0:1, lanes] = p0 * self_c + p1 * mix_s
        qv[1:2, lanes] = p0 * low_pos
        qv[2:3, lanes] = -p0 * jnp.minimum(rise_s, 0.0)
        qv[3:4, lanes] = p0 * left_pos
        qv[4:5, lanes] = -p0 * jnp.minimum(cross_s, 0.0)
        return 0

    def q_copy(to):
        return rcopy(qv, qv, s_q.at[to], r_q.at[0], {"lev": to})

    @pl.when(l == 0)
    def _():
        qv[...] = jnp.zeros_like(qv)
        lax.fori_loop(0, S // CH, q_step, 0)

        def q_send(d, _):
            q_copy(lax.rem(l + d, NL)).start()
            return 0

        lax.fori_loop(1, NL, q_send, 0)

    for c in planes:
        c.wait_recv()
    mx[0] = mx[0] * jnp.where(l == 0, 0.0, 1.0).astype(f32)

    def shifted(get, i, lo_row, hi_row):
        c = get(8 * i, 8)
        lower = jnp.concatenate([lo_row, c[:7]], axis=0) if i == 0 else get(8 * i - 1, 8)
        upper = jnp.concatenate([c[1:], hi_row], axis=0) if i == R // 8 - 1 else get(8 * i + 1, 8)
        return c, lower, upper

    def stencil(k, get, get_above, get_below, lo_row, hi_row, adjoint, put):
        rl = rb0lo[pl.ds(8 + k, 1), :]
        for i in range(R // 8):
            c, lower, upper = shifted(get, i, lo_row, hi_row)
            rows = pl.ds(8 * i, 8)
            rise = wr[k, rows, :]
            if i == 0:
                rise_low = jnp.concatenate([rl, rise[:7]], axis=0)
            else:
                rise_low = wr[k, pl.ds(8 * i - 1, 8), :]
            cross = wc[k, rows, :]
            cross_left = jnp.roll(cross, 1, axis=1)
            right = jnp.roll(c, -1, axis=1)
            left = jnp.roll(c, 1, axis=1)
            m = mx[k + 1, rows, :]
            ml = mx[k, rows, :]
            above = get_above(8 * i)
            below = get_below(8 * i)
            if adjoint:
                v = jnp.maximum(rise, 0.0) * (upper - c) - jnp.minimum(rise_low, 0.0) * (lower - c)
                v += jnp.maximum(cross, 0.0) * (right - c) - jnp.minimum(cross_left, 0.0) * (left - c)
            else:
                v = jnp.maximum(rise_low, 0.0) * lower + jnp.minimum(rise_low, 0.0) * c
                v -= jnp.maximum(rise, 0.0) * c + jnp.minimum(rise, 0.0) * upper
                v += jnp.maximum(cross_left, 0.0) * left + jnp.minimum(cross_left, 0.0) * c
                v -= jnp.maximum(cross, 0.0) * c + jnp.minimum(cross, 0.0) * right
            v = c + v + m * (above - c) - ml * (c - below)
            put(rows, v)

    def at_level(ref, k):
        return lambda o, n=8: ref[k, pl.ds(o, n), 0:C]

    def fwd1(k, _):
        def put(rows, v):
            s1[k + 1, rows, :] = v

        stencil(
            k, at_level(t_v, k + 1), at_level(t_v, k + 2), at_level(t_v, k),
            rb0lo[pl.ds(k, 1), :], rb0hi[pl.ds(k, 1), :], False, put,
        )
        return 0

    lax.fori_loop(0, L, fwd1, 0)
    s1[0] = jnp.zeros((R, C), f32)
    s1[L + 1] = jnp.zeros((R, C), f32)

    def a2a_wait(d, _):
        src = lax.rem(t + d, NT)
        i_copy(src, src).wait_recv()
        a_copy(src, src).wait_recv()
        return 0

    lax.fori_loop(1, NT, a2a_wait, 0)
    got_id = rid[...].reshape(NT, 128)
    per = NT // NG
    id_rows = [
        jnp.sum(got_id[g * per : (g + 1) * per], axis=0, keepdims=True)[:, :LG] - 1.0 for g in range(NG)
    ]
    id_row = jnp.concatenate(id_rows, axis=1)
    owner = jnp.where(iota((NB, SL), 0).astype(f32) == id_row, 1.0, 0.0).astype(bf16)
    rh, rl_ = split2(rbuf[...].reshape(SL, 128))
    blk[...] = dot(owner, rh) + dot(owner, rl_)
    NGR = R // 8
    per_g = NB // NGR
    for r in range(8):
        q, o = divmod(C * r, 128)
        width = min(per_g - q, C // 128 + 2)
        parts = [blk[pl.ds(q + i, NGR, stride=per_g), :] for i in range(width)]
        while len(parts) < C // 128 + 2:
            parts.append(jnp.zeros((NGR, 128), f32))
        v = jnp.concatenate(parts, axis=1)
        if o:
            v = pltpu.roll(v, v.shape[1] - o, 1)
        for j in range(surf6.shape[0]):
            surf6.at[j][pl.ds(r, NGR, stride=8), :] = v[:, 128 * j : 128 * j + 128]
    surf = jnp.concatenate([surf6[j] for j in range(surf6.shape[0])], axis=1)[:, :C]
    pk1u[...] = jnp.zeros_like(pk1u)
    pk1d[...] = jnp.zeros_like(pk1d)
    for k in range(L):
        pk1u[k : k + 1, :] = s1[k + 1, R - 1 : R, :]
        pk1d[k : k + 1, :] = s1[k + 1, 0:1, :]
    pk1u[L : L + 1, :] = surf[R - 1 : R]
    pk1d[L : L + 1, :] = surf[0:1]
    rows1 = pair_copies(pk1u, pk1d, rb1lo, rb1hi, s_r1, r_r1)
    for c in rows1:
        c.start()

    GT = (L + 2) * R + RS + 2 * R
    o_s = (L + 2) * R
    put_g(0, mx[0] * s1[1], GT)
    put_g((L + 1) * R, mx[L] * s1[L], GT)
    put_g(o_s + RS, jnp.roll(surf, 1, axis=1), GT)
    put_g(o_s + RS + R, jnp.roll(surf, -1, axis=1), GT)
    for c in rows1:
        c.wait_recv()
    put_g(o_s, jnp.concatenate([rb1lo[L : L + 1, :], surf, rb1hi[L : L + 1, :], jnp.zeros((14, C), f32)], axis=0), GT)

    def fwd2(k, _):
        def put(rows, v):
            s2[rows, :] = v

        stencil(
            k, at_level(s1, k + 1), at_level(s1, k + 2), at_level(s1, k),
            rb1lo[pl.ds(k, 1), :], rb1hi[pl.ds(k, 1), :], False, put,
        )
        hi, lo = split2(s2[...])
        gmat[pl.ds(pl.multiple_of((k + 1) * R, 16), R), :] = hi
        gmat[pl.ds(pl.multiple_of(GT + (k + 1) * R, 16), R), :] = lo
        return 0

    lax.fori_loop(0, L, fwd2, 0)

    @pl.when(l != 0)
    def _():
        q_copy(0).wait_recv()

    def coef_of(r, lanes, scale):
        c = jnp.where(idx == r + 1, scale * qv[0:1, lanes], 0.0)
        c += jnp.where(idx == r, scale * qv[1:2, lanes], 0.0)
        return c + jnp.where(idx == r + 2, scale * qv[2:3, lanes], 0.0)

    def gather_step(j, _):
        lanes = pl.ds(pl.multiple_of(j * CH, CH), CH)
        v2 = dot(gmat[0 : 2 * GT, :], ct[0:C, lanes])
        v = v2[:GT] + v2[GT:]
        r = rowi[:, lanes]
        acc = qv[3:4, lanes] * v[o_s + RS : o_s + RS + R] + qv[4:5, lanes] * v[o_s + RS + R : GT]
        for k in range(L + 2):
            acc += w8[k : k + 1, lanes] * v[k * R : (k + 1) * R]
        part = jnp.sum(jnp.where(idr == r, acc, 0.0), axis=0, keepdims=True)
        part += jnp.sum(v[o_s : o_s + RS] * coef_of(r, lanes, 1.0), axis=0, keepdims=True)
        slope_v[:, lanes] = part
        return 0

    lax.fori_loop(0, S // CH, gather_step, 0)
    cbuf[l] = slope_v[...]

    def c_copy(to, slot):
        return rcopy(slope_v, cbuf.at[slot], s_c.at[to], r_c.at[slot], {"lev": to})

    def c_send(d, _):
        c_copy(lax.rem(l + d, NL), l).start()
        return 0

    def c_wait(d, _):
        src = lax.rem(l + d, NL)
        c_copy(src, src).wait_recv()
        return 0

    def c_sent(d, _):
        c_copy(lax.rem(l + d, NL), l).wait_send()
        return 0

    lax.fori_loop(1, NL, c_send, 0)
    lax.fori_loop(1, NL, c_wait, 0)
    column = cbuf[0]
    for i in range(1, NL):
        column = column + cbuf[i]
    live = iota((1, S), 1) < cnt[...]
    modeled[...] = jnp.where(live, column, 0.0)
    sigma = ssig[...]
    scaled = (column - sobs[...]) / sigma
    size_abs = jnp.abs(scaled)
    misfit[...] = jnp.where(live, jnp.where(size_abs <= 1.0, 0.5 * scaled * scaled, size_abs - 0.5), 0.0)
    slope = jnp.where(live, jnp.clip(scaled, -1.0, 1.0) / sigma, 0.0)
    lax.fori_loop(1, NL, c_sent, 0)
    slope_v[...] = slope

    def put_a(at, lanes, value):
        n = value.shape[0]
        hi, lo = split2(value)
        amat[at : at + n, lanes] = hi
        amat[GT + at : GT + at + n, lanes] = lo

    def a_step(j, _):
        lanes = pl.ds(pl.multiple_of(j * CH, CH), CH)
        r = rowi[:, lanes]
        sl = slope_v[:, lanes]
        mine = idr == r
        for k in range(L + 2):
            put_a(k * R, lanes, jnp.where(mine, sl * w8[k : k + 1, lanes], 0.0))
        put_a(o_s, lanes, coef_of(r, lanes, sl))
        put_a(o_s + RS, lanes, jnp.where(mine, sl * qv[3:4, lanes], 0.0))
        put_a(o_s + RS + R, lanes, jnp.where(mine, sl * qv[4:5, lanes], 0.0))
        return 0

    lax.fori_loop(0, S // CH, a_step, 0)

    def scatter_step(j, _):
        off = pl.multiple_of(j * CH, CH)
        v2 = dot_nt(amat[...], ct[pl.ds(off, CH), :])
        v = v2[:GT] + v2[GT:]
        a2[:, :, pl.ds(off, CH)] = v[:o_s].reshape(L + 2, R, CH)
        bs[:, pl.ds(off, CH)] = v[o_s:]
        return 0

    lax.fori_loop(0, ct.shape[0] // CH, scatter_step, 0)
    pk2u[...] = jnp.zeros_like(pk2u)
    pk2d[...] = jnp.zeros_like(pk2d)
    for k in range(L):
        pk2u[k : k + 1, :] = a2[k + 1, R - 1 : R, 0:C]
        pk2d[k : k + 1, :] = a2[k + 1, 0:1, 0:C]
    pk2u[L : L + 1, :] = bs[R + 1 : R + 2, 0:C]
    pk2d[L : L + 1, :] = bs[0:1, 0:C]
    rows2 = pair_copies(pk2u, pk2d, rb2lo, rb2hi, s_r2, r_r2)
    for c in rows2:
        c.start()
    bar = bs[1 : R + 1, 0:C]
    bar += jnp.roll(bs[RS : RS + R, 0:C], -1, axis=1) + jnp.roll(bs[RS + R : RS + 2 * R, 0:C], 1, axis=1)
    for c in rows2:
        c.wait_recv()

    def adj1(k):
        def put(rows, v):
            a1[k + 1, rows, :] = v

        stencil(
            k, at_level(a2, k + 1), at_level(a2, k + 2), at_level(a2, k),
            rb2lo[pl.ds(k, 1), :], rb2hi[pl.ds(k, 1), :], True, put,
        )

    def adj1_step(k, _):
        adj1(k)
        return 0

    def adj1_ends(i, _):
        adj1(i * (L - 1))
        return 0

    lax.fori_loop(0, 2, adj1_ends, 0)
    planes1 = [
        rcopy(a1.at[L], a1.at[0], s_l1.at[0], r_l1.at[0], {"lev": lup}),
        rcopy(a1.at[1], a1.at[L + 1], s_l1.at[1], r_l1.at[1], {"lev": ldn}),
    ]

    rid_ = iota((R, C), 0)
    bar += jnp.where(rid_ == 0, rb2lo[L : L + 1, :], 0.0) + jnp.where(rid_ == R - 1, rb2hi[L : L + 1, :], 0.0)
    wide = jnp.concatenate([bar, jnp.zeros((R, 128 * surf6.shape[0] - C), f32)], axis=1)
    for j in range(surf6.shape[0]):
        surf6[j] = wide[:, 128 * j : 128 * j + 128]
    lines = []
    for r in range(8):
        lines.append(
            jnp.concatenate(
                [surf6.at[j][pl.ds(r, NGR, stride=8), :] for j in range(surf6.shape[0])], axis=1
            )
        )
    for q in range(per_g):
        r, c = divmod(128 * q, C)
        if c + 128 <= C:
            piece = lines[r][:, c : c + 128]
        else:
            piece = jnp.concatenate([lines[r][:, c:C], lines[r + 1][:, : c + 128 - C]], axis=1)
        blk[pl.ds(q, NGR, stride=per_g), :] = piece
    bh, bl = split2(blk[...])
    for g in range(NG):
        spread = jnp.broadcast_to(id_rows[g], (128, LG)).T
        want = jnp.concatenate([spread] * (-(-NB // 128)), axis=1)[:, :NB]
        mine = jnp.where(iota((LG, NB), 1).astype(f32) == want, 1.0, 0.0).astype(bf16)
        back = dot(mine, bh) + dot(mine, bl)
        bout[g * per : (g + 1) * per] = back.reshape(per, SLOT, 128)

    def b_copy(to, slot):
        return rcopy(bout.at[to], bin_.at[slot], s_b.at[to], r_b.at[slot], {"tile": to})

    def b_send(d, _):
        b_copy(lax.rem(t + d, NT), t).start()
        return 0

    lax.fori_loop(1, NT, b_send, 0)
    bin_[t] = bout[t]
    for c in planes1:
        c.start()
    lax.fori_loop(1, L - 1, adj1_step, 0)
    pk3u[...] = jnp.zeros_like(pk3u)
    pk3d[...] = jnp.zeros_like(pk3d)
    for k in range(L):
        pk3u[k : k + 1, :] = a1[k + 1, R - 1 : R, :]
        pk3d[k : k + 1, :] = a1[k + 1, 0:1, :]
    rows3 = pair_copies(pk3u, pk3d, rb3lo, rb3hi, s_r3, r_r3)
    for c in rows3:
        c.start()

    def b_wait(d, _):
        src = lax.rem(t + d, NT)
        b_copy(src, src).wait_recv()
        return 0

    lax.fori_loop(1, NT, b_wait, 0)
    take = jnp.where(iota((NE, SL), 1) == sel_col, 1.0, 0.0).astype(bf16)
    gh, gl = split2(bin_[...].reshape(SL, 128))
    picked[...] = dot(take, gh) + dot(take, gl)

    def fgrad_step(i, _):
        outs = []
        for p in range(CPG):
            f = i * CPG + p
            row = jnp.concatenate([picked[pl.ds(2 * f, 1), :], picked[pl.ds(2 * f + 1, 1), :]], axis=1)
            fh = row.astype(bf16).astype(f32)
            both = jnp.where(r16 == 0, fh, jnp.where(r16 == 1, row - fh, 0.0)).astype(bf16)
            got = dot(both, wcat[f])
            outs.append(got[0:1, :128] + got[0:1, 128:] + got[1:2, :128])
        for p in range(CPG):
            fgrad[pl.ds(i * CPG + p, 1), :] = outs[p]
        return 0

    lax.fori_loop(0, NCH, fgrad_step, 0)

    for c in rows3:
        c.wait_recv()
    for c in planes1:
        c.wait_recv()

    def grad_step(k, _):
        def put(rows, v):
            grad[k, rows, :] = v

        stencil(
            k, at_level(a1, k + 1), at_level(a1, k + 2), at_level(a1, k),
            rb3lo[pl.ds(k, 1), :], rb3hi[pl.ds(k, 1), :], True, put,
        )
        return 0

    lax.fori_loop(0, L, grad_step, 0)

    for c in planes + rows0 + rows1 + rows2 + planes1 + rows3:
        c.wait_send()

    def lev_sent(d, _):
        prof_copy(lax.rem(l + d, NL), l).wait_send()
        return 0

    lax.fori_loop(1, NL, lev_sent, 0)

    @pl.when(l == 0)
    def _():
        def q_sent(d, _):
            q_copy(lax.rem(l + d, NL)).wait_send()
            return 0

        lax.fori_loop(1, NL, q_sent, 0)

    def tile_sent(d, _):
        to = lax.rem(t + d, NT)
        i_copy(to, t).wait_send()
        a_copy(to, t).wait_send()
        b_copy(to, t).wait_send()
        return 0

    lax.fori_loop(1, NT, tile_sent, 0)


def on_device(NT, NL, tr, wr, wc, df, flux, w, rtile, rblock, profiles, cnt, scol, sprof, sobs, ssig):
    L, R, C = tr.shape
    NE = w.shape[0]
    S = scol.shape[0]
    NP = NE // 2
    CPG = 5 if NP % 5 == 0 else 1
    SL = NT * SLOT
    NB = R * C // 128
    CP = -(-C // 256) * 256
    CK = -(-C // 128)
    RS = R + 16
    GT = (L + 2) * R + RS + 2 * R
    any_, vm = pl.BlockSpec(memory_space=pl.ANY), pl.BlockSpec(memory_space=pltpu.VMEM)
    V = pltpu.VMEM
    D = pltpu.SemaphoreType.DMA
    scratch = [
        V((L + 2, R, C), f32), V((L, R, C), f32), V((L, R, C), f32), V((L + 1, R, C), f32),
        V(w.shape, f32), V((NP, 256, 256), bf16), V((NE, 128), f32),
        V((NT, SLOT, 128), f32), V((NT, SLOT, 128), f32), V((NT, 1, 128), f32), V((NT, 1, 128), f32),
        V((NL, 8, 128), f32),
        V((16, C), f32), V((8, C), f32), V((16, C), f32), V((8, C), f32),
        V((8, C), f32), V((8, C), f32), V((8, C), f32), V((8, C), f32),
        V((8, C), f32), V((8, C), f32), V((8, C), f32), V((8, C), f32),
        V((8, C), f32), V((8, C), f32), V((8, C), f32), V((8, C), f32),
        V((CP, S), bf16), V((2 * GT, S), bf16), V((2 * GT, C), bf16),
        V((L + 2, R, C), f32), V((R, C), f32), V((1, S), jnp.int32), V((8, S), f32), V((8, S), f32),
        V((NL, 1, S), f32), V((1, S), f32), V((L + 2, R, CP), f32), V((RS + 2 * R, CP), f32),
        V((L + 2, R, C), f32), V((CK, R, 128), f32), V((NB, 128), f32),
        V((NT, SLOT, 128), f32), V((NT, SLOT, 128), f32), V((NE, 128), f32),
        D((4 + NP // CPG,)), D((3,)), D((3,)), D((NL,)), D((NL,)), D((2,)), D((2,)),
        D((NT,)), D((NT,)), D((NT,)), D((NT,)), D((NL,)), D((1,)),
        D((2,)), D((2,)), D((NL,)), D((NL,)), D((2,)), D((2,)), D((2,)), D((2,)), D((2,)), D((2,)),
        D((NT,)), D((NT,)),
    ]
    prof = jnp.pad(profiles.T, ((0, 8 - L), (0, 128 - profiles.shape[0])))
    modeled, misfit, grad, fgrad = pl.pallas_call(
        functools.partial(body, (NT, NL, L, R, C, S, NE, CPG)),
        out_shape=[
            jax.ShapeDtypeStruct((1, S), f32),
            jax.ShapeDtypeStruct((1, S), f32),
            jax.ShapeDtypeStruct((L, R, C), f32),
            jax.ShapeDtypeStruct((NP, 128), f32),
        ],
        in_specs=[any_] * 5 + [vm] * 10,
        out_specs=[vm] * 4,
        scratch_shapes=scratch,
        compiler_params=pltpu.CompilerParams(
            collective_id=0, has_side_effects=True, vmem_limit_bytes=63000 * 1024
        ),
    )(
        tr, wr, wc, df, w, flux, rtile, rtile.reshape(1, NE), rblock.reshape(1, NE), prof,
        cnt.reshape(1, 1), scol.reshape(1, S), sprof.reshape(1, S), sobs.reshape(1, S), ssig.reshape(1, S),
    )
    return modeled.reshape(S), misfit.reshape(S), grad, fgrad


def solution(mesh):
    both = ("tile", "lev")
    field = P("lev", "tile", None)
    in_specs = (
        field, field, field, field, P(both, None), P(both, None, None), P(both, None), P(both),
        P(None, "lev"), P("tile"), P("tile"), P("tile"), P("tile"), P("tile"),
    )
    out_specs = (P("tile"), P("tile"), field, P(both, None))
    return jax.shard_map(
        functools.partial(on_device, mesh.shape["tile"], mesh.shape["lev"]),
        mesh=mesh, in_specs=in_specs, out_specs=out_specs, check_vma=False,
    )
```
